32 devices in a mesh: segment: 16 (over z, x, core), slab: 2 (over y).
Axes of the slice: x: 2, y: 2, z: 4, core: 2. Of those that a mesh axis runs over, the one named last changes fastest.
Arguments:
- fwd_in: bfloat16 [16, 2, 32, 4, 4, 128], P('segment', None, None, 'slab'), may hold values from -6 to 6
- back_out: bfloat16 [16, 2, 32, 4, 4, 128], P('segment', None, None, 'slab'), may hold values from -6 to 6
- back_grad: bfloat16 [16, 2, 32, 4, 4, 128], P('segment', None, None, 'slab'), may hold values from -6 to 6
- batch_next: bfloat16 [2, 32, 4, 4, 128], P(None, None, 'slab'), may hold values from -6 to 6
- loss_grad: bfloat16 [2, 2, 32, 4, 4, 128], P(None, None, None, 'slab'), may hold values from -6 to 6
- weights: bfloat16 [16, 2, 32, 864], P('segment'), may hold values from -0.21875 to 0.21875
Outputs:
- fwd_out: bfloat16 [16, 2, 32, 4, 4, 128], P('segment', None, None, 'slab')
- back_acts: bfloat16 [16, 2, 32, 4, 4, 128], P('segment', None, None, 'slab')
- back_grads: bfloat16 [16, 2, 32, 4, 4, 128], P('segment', None, None, 'slab')
- weight_grads: float32 [16, 2, 32, 864], P('segment', None, None, 'slab')
The draws below stay inside these ranges and needn't reach their ends.
All inputs are finite; a program needn't handle non-finite values.
Results may differ from the reference program's by a relative error of at most 0.012.
Values may be sent and summed in bfloat16 or wider, within the bound.
A program may use at most 64 MiB of HBM per device.

```python
import jax
import jax.numpy as jnp
from jax import lax

C = 32
PLANE_H = 4
PLANE_W = 128
SEGMENTS = 16
DEPTH = 4
CELLS = 2048


def steps_of(key, dims, cuts, least, high):
    gain = 1.0
    for dim, parts in cuts:
        steps = jax.random.uniform(jax.random.fold_in(jax.random.fold_in(key, 6), dim), (parts,), jnp.float32, least / len(cuts), high / len(cuts))
        gain = gain * jnp.repeat(jnp.exp(steps), dims[dim] // parts).reshape((-1,) + (1,) * (len(dims) - 1 - dim))
    return gain


def noise(rng, dims, scale, bound, split=(), kind=jnp.bfloat16):
    array = scale * jax.random.normal(rng, dims, jnp.float32)
    if split:
        array = array * steps_of(rng, dims, split, -0.22, 0.18)
    return jnp.clip(array, -bound, bound).astype(kind)


def setup_inputs(seed: int = 0) -> dict:
    streams_of = jax.random.split(jax.random.key(seed), 7)
    return {
        "fwd_in": noise(streams_of[0], (SEGMENTS, 2, C, DEPTH, PLANE_H, PLANE_W), 1.0, 6.0, ((0, 16), (3, 2))),
        "back_out": noise(streams_of[1], (SEGMENTS, 2, C, DEPTH, PLANE_H, PLANE_W), 1.0, 6.0, ((0, 16), (3, 2))),
        "back_grad": noise(streams_of[2], (SEGMENTS, 2, C, DEPTH, PLANE_H, PLANE_W), 1.0, 6.0, ((0, 16), (3, 2))),
        "batch_next": noise(streams_of[3], (2, C, DEPTH, PLANE_H, PLANE_W), 1.0, 6.0, ((2, 2),)),
        "loss_grad": noise(streams_of[4], (2, 2, C, DEPTH, PLANE_H, PLANE_W), 1.0, 6.0, ((3, 2),)),
        "weights": noise(streams_of[5], (SEGMENTS, 2, C, 27 * C), (27 * C) ** -0.5, 0.21875, ((0, 16),)),
    }


def silu_round(value):
    return jax.nn.silu(value.astype(jnp.float32)).astype(jnp.bfloat16)

def silu_slope(value):
    wide = value.astype(jnp.float32)
    sig = jax.nn.sigmoid(wide)
    return sig * (1.0 + wide * (1.0 - sig))

def kernel_of(flat):
    chan = flat.shape[0]
    return flat.reshape(chan, chan, 3, 3, 3)

def conv_full(field, flat):
    out = lax.conv_general_dilated(field[None], kernel_of(flat), (1, 1, 1), ((1, 1), (1, 1), (1, 1)), dimension_numbers=('NCDHW', 'OIDHW', 'NCDHW'), preferred_element_type=jnp.float32)
    return out[0]

def conv_back(grad, flat):
    turned = jnp.flip(kernel_of(flat), (2, 3, 4)).transpose(1, 0, 2, 3, 4)
    out = lax.conv_general_dilated(grad[None], turned, (1, 1, 1), ((1, 1), (1, 1), (1, 1)), dimension_numbers=('NCDHW', 'OIDHW', 'NCDHW'), preferred_element_type=jnp.float32)
    return out[0]

def weight_grad(grad, field):
    padded = jnp.pad(field, ((0, 0), (1, 1), (1, 1), (1, 1)))
    out = lax.conv_general_dilated(padded[:, None], grad[:, None], (1, 1, 1), 'VALID', dimension_numbers=('NCDHW', 'OIDHW', 'NCDHW'), preferred_element_type=jnp.float32)
    out = out.transpose(1, 0, 2, 3, 4)
    return out.reshape(out.shape[0], -1)

def section(inputs):
    fin, back_pair, back_cot, wts = inputs
    x1 = fin[0]
    x2 = fin[1]
    y1 = (x1.astype(jnp.float32) + conv_full(silu_round(x2), wts[0])).astype(jnp.bfloat16)
    y2 = (x2.astype(jnp.float32) + conv_full(silu_round(y1), wts[1])).astype(jnp.bfloat16)
    out1 = back_pair[0]
    out2 = back_pair[1]
    grad1 = back_cot[0]
    grad2 = back_cot[1]
    hidden = silu_round(out1)
    rec2 = (out2.astype(jnp.float32) - conv_full(hidden, wts[1])).astype(jnp.bfloat16)
    act2 = silu_round(rec2)
    rec1 = (out1.astype(jnp.float32) - conv_full(act2, wts[0])).astype(jnp.bfloat16)
    grad_one = (grad1.astype(jnp.float32) + silu_slope(out1) * conv_back(grad2, wts[1])).astype(jnp.bfloat16)
    grad_two = (grad2.astype(jnp.float32) + silu_slope(rec2) * conv_back(grad_one, wts[0])).astype(jnp.bfloat16)
    scale = float(CELLS) ** (-0.5)
    dweights = jnp.stack([weight_grad(grad_one, act2), weight_grad(grad2, hidden)]) * scale
    return (jnp.stack([y1, y2]), jnp.stack([rec1, rec2]), jnp.stack([grad_one, grad_two]), dweights)

def reference(fwd_in, back_out, back_grad, batch_next, loss_grad, weights):
    fout1, rec1, din1, dw1 = lax.map(section, (fwd_in, back_out, back_grad, weights))
    fin2 = jnp.concatenate([batch_next[None], fout1[:-1]], axis=0)
    acts2 = jnp.concatenate([rec1[1:], fout1[-1:]], axis=0)
    grads2 = jnp.concatenate([din1[1:], loss_grad[0][None]], axis=0)
    fout2, rec2, din2, dw2 = lax.map(section, (fin2, acts2, grads2, weights))
    back_acts = jnp.concatenate([rec2[1:], fout2[-1:]], axis=0)
    back_grads = jnp.concatenate([din2[1:], loss_grad[1][None]], axis=0)
    return (fout2, back_acts, back_grads, dw1 + dw2)
```

```python
import functools

import jax
import jax.numpy as jnp
from jax import lax
from jax.experimental import pallas as pl
from jax.experimental.pallas import tpu as pltpu
from jax.sharding import PartitionSpec as P

MESH = pl.DeviceIdType.MESH
F, G, FT, GT = range(4)
X1, X2, O1, O2, G1, G2 = range(6)
Y1, Y2, R1, R2, E1, E2 = range(6)
PX, PH, PD, PY, PU, PE = range(6)


def sigmoid(v):
    return 1.0 / (1.0 + jnp.exp(-v))


def silu(v):
    return v / (1.0 + jnp.exp(-v))


def slope(v):
    sig = sigmoid(v)
    return sig * (1.0 + v * (1.0 - sig))


def kernel(
    dims, fwd, bout, bgrad, nxt, loss, w, fout, backs, grads, dw,
    pad, stage, second, made, nat, acc, g3, dsum, dpart, dgot,
    halo_s, halo_r, seg_s, seg_r, out_s, d_s, d_r,
):
    C, D, H, W, segs, n, scale = dims
    DH, HW = D * H, H * W
    cs = C // n
    f32, bf16 = jnp.float32, jnp.bfloat16
    seg = lax.axis_index("segment")
    slab = lax.axis_index("slab")
    has_prev, has_next = seg > 0, seg < segs - 1
    is_first, is_last = seg == 0, seg == segs - 1
    prev_seg = lax.rem(seg + segs - 1, segs)
    next_seg = lax.rem(seg + 1, segs)
    lane_no = lax.broadcasted_iota(jnp.int32, (C, W), 1)

    barrier = pltpu.get_barrier_semaphore()

    @pl.when(has_prev)
    def _():
        pl.semaphore_signal(barrier, inc=1, device_id={"segment": prev_seg}, device_id_type=MESH)

    @pl.when(has_next)
    def _():
        pl.semaphore_signal(barrier, inc=1, device_id={"segment": next_seg}, device_id_type=MESH)

    for k in range(1, n):
        pl.semaphore_signal(
            barrier, inc=1, device_id={"slab": lax.rem(slab + k, n)}, device_id_type=MESH
        )

    def lane(q, hh):
        return (q * (H + 2) + hh) * W

    zero = jnp.zeros((C, W), bf16)
    for t in range(2):
        for k in range(6):
            for q in range(D + 2):
                for hh in (0, H + 1):
                    pad[t, k, :, pl.ds(lane(q, hh), W)] = zero

    @pl.when(slab == 0)
    def _():
        for t in range(2):
            for k in range(6):
                pad[t, k, :, pl.ds(lane(0, 1), HW)] = jnp.zeros((C, HW), bf16)

    @pl.when(slab == n - 1)
    def _():
        for t in range(2):
            for k in range(6):
                pad[t, k, :, pl.ds(lane(D + 1, 1), HW)] = jnp.zeros((C, HW), bf16)

    def load_stage(slot, ref, s):
        stage[slot] = ref[s].astype(f32)

    def staged(slot, r):
        return stage[slot, pl.ds(r, C, stride=DH), :]

    for s in range(2):
        load_stage(G1 + s, bgrad, s)
        load_stage(O1 + s, bout, s)
        load_stage(X1 + s, fwd, s)

    def halo(t, k, up):
        src_q, dst_q = (D, 0) if up else (1, D + 1)
        target = lax.rem(slab + (1 if up else n - 1), n)
        return pltpu.make_async_remote_copy(
            src_ref=pad.at[t, k, :, pl.ds(lane(src_q, 1), HW)],
            dst_ref=pad.at[t, k, :, pl.ds(lane(dst_q, 1), HW)],
            send_sem=halo_s.at[t, k, up],
            recv_sem=halo_r.at[t, k, up],
            device_id={"slab": target},
            device_id_type=MESH,
        )

    def halo_start(t, k):
        @pl.when(slab < n - 1)
        def _():
            halo(t, k, 1).start()

        @pl.when(slab > 0)
        def _():
            halo(t, k, 0).start()

    def halo_arrived(t, k):
        @pl.when(slab > 0)
        def _():
            halo(t, k, 1).wait_recv()

        @pl.when(slab < n - 1)
        def _():
            halo(t, k, 0).wait_recv()

    def halo_sent(t, k):
        @pl.when(slab < n - 1)
        def _():
            halo(t, k, 1).wait_send()

        @pl.when(slab > 0)
        def _():
            halo(t, k, 0).wait_send()

    def to_next(k):
        return pltpu.make_async_remote_copy(
            src_ref=made.at[0, k], dst_ref=second.at[X1 + k],
            send_sem=seg_s.at[0, k], recv_sem=seg_r.at[0, k],
            device_id={"segment": next_seg}, device_id_type=MESH,
        )

    def to_prev(k):
        return pltpu.make_async_remote_copy(
            src_ref=made.at[0, k], dst_ref=second.at[k],
            send_sem=seg_s.at[0, k], recv_sem=seg_r.at[0, k],
            device_id={"segment": prev_seg}, device_id_type=MESH,
        )

    def out_prev(k):
        dst = backs.at[k - R1] if k < E1 else grads.at[k - E1]
        return pltpu.make_async_remote_copy(
            src_ref=nat.at[k], dst_ref=dst,
            send_sem=seg_s.at[1, k], recv_sem=seg_r.at[1, k],
            device_id={"segment": prev_seg}, device_id_type=MESH,
        )

    def own_out(k):
        return pltpu.make_async_copy(nat.at[k], fout.at[k], out_s.at[k])

    def last_act(k):
        return pltpu.make_async_copy(nat.at[k], backs.at[k], out_s.at[2 + k])

    def last_grad(k):
        return pltpu.make_async_copy(loss.at[2 + k], grads.at[k], out_s.at[4 + k])

    def put(t, k, r, value):
        d, h = divmod(r, H)
        pad[t, k, :, pl.ds(lane(d + 1, h + 1), W)] = value.astype(bf16)

    def tall(t, k, q):
        return jnp.concatenate([pad[t, k, :, pl.ds(lane(q, b), HW)] for b in range(3)], axis=0)

    def conv_local(t, k, m, slot):
        for p in range(D):
            total = None
            for a in range(3):
                if 1 <= p + a <= D:
                    part = jnp.dot(w[m, a], tall(t, k, p + a), preferred_element_type=f32)
                    total = part if total is None else total + part
            acc[slot, :, pl.ds(p * HW, HW)] = total

    def conv_finish(t, k, m, slot):
        for p in range(D):
            total = acc[slot, :, pl.ds(p * HW, HW)]
            for a in range(3):
                if not 1 <= p + a <= D:
                    total += jnp.dot(w[m, a], tall(t, k, p + a), preferred_element_type=f32)
            for h in range(H):
                y = total[:, h * W : (h + 1) * W]
                left = jnp.where(lane_no == 0, 0.0, pltpu.roll(y[:C], 1, 1))
                right = jnp.where(lane_no == W - 1, 0.0, pltpu.roll(y[2 * C :], W - 1, 1))
                yield p * H + h, y[C : 2 * C] + left + right

    def widen(j, r, v):
        at = pl.ds(r * W, W)
        g3[j, 0:C, at] = jnp.where(lane_no == W - 1, 0.0, pltpu.roll(v, W - 1, 1)).astype(bf16)
        g3[j, C : 2 * C, at] = v.astype(bf16)
        g3[j, 2 * C : 3 * C, at] = jnp.where(lane_no == 0, 0.0, pltpu.roll(v, 1, 1)).astype(bf16)

    def wgrad(t, k, j):
        total = None
        for p in range(D):
            lhs = jnp.concatenate([tall(t, k, p + a) for a in range(3)], axis=0)
            part = lax.dot_general(
                lhs, g3[j, :, pl.ds(p * HW, HW)], (((1,), (1,)), ((), ())),
                preferred_element_type=f32,
            )
            total = part if total is None else total + part
        if t == 0:
            dsum[j] = total
            return
        total += dsum[j]
        for q in range(n):
            for ab in range(9):
                dpart[j, q, ab] = total[ab * C + q * cs : ab * C + (q + 1) * cs]
        for q in range(1, n):
            share(j, q).start()

    def share(j, q):
        target = lax.rem(slab + q, n)
        return pltpu.make_async_remote_copy(
            src_ref=dpart.at[j, target], dst_ref=dgot.at[j, q],
            send_sem=d_s.at[j, q], recv_sem=d_r.at[j, q],
            device_id={"slab": target}, device_id_type=MESH,
        )

    def keep(t, k, r, value):
        held = value.astype(bf16)
        made[t, k, :, pl.ds(r * W, W)] = held
        wide = held.astype(f32)
        if t == 1:
            stage[k, pl.ds(r, C, stride=DH), :] = wide
        return wide

    def send_made(t, k):
        if t == 0:
            if k < R1:
                @pl.when(has_next)
                def _():
                    to_next(k).start()

                @pl.when(is_last)
                def _():
                    second[O1 + k] = made[0, k]
            else:
                @pl.when(has_prev)
                def _():
                    to_prev(k).start()
            return
        nat[k] = stage[k].astype(bf16)
        if k < R1:
            own_out(k).start()

            @pl.when(is_last)
            def _():
                last_act(k).start()
        else:
            @pl.when(has_prev)
            def _():
                out_prev(k).start()

    def tick(t, get, ready):
        ready(G2)
        for r in range(DH):
            put(t, PD, r, get(G2, r))
        if t == 0:
            peers = has_prev.astype(jnp.int32) + has_next.astype(jnp.int32) + n - 1
            pl.semaphore_wait(barrier, peers)
        halo_start(t, PD)
        ready(O1)
        for r in range(DH):
            put(t, PH, r, silu(get(O1, r)))
        halo_start(t, PH)
        ready(X2)
        for r in range(DH):
            put(t, PX, r, silu(get(X2, r)))
        halo_start(t, PX)
        conv_local(t, PD, GT, 0)
        conv_local(t, PH, G, 1)
        conv_local(t, PX, F, 2)
        for r in range(DH):
            widen(1, r, get(G2, r))

        ready(G1)
        halo_arrived(t, PD)
        for r, out in conv_finish(t, PD, GT, 0):
            put(t, PE, r, keep(t, E1, r, get(G1, r) + slope(get(O1, r)) * out))
        halo_start(t, PE)
        send_made(t, E1)
        ready(O2)
        halo_arrived(t, PH)
        for r, out in conv_finish(t, PH, G, 1):
            put(t, PU, r, silu(keep(t, R2, r, get(O2, r) - out)))
        halo_start(t, PU)
        send_made(t, R2)
        ready(X1)
        halo_arrived(t, PX)
        for r, out in conv_finish(t, PX, F, 2):
            put(t, PY, r, silu(keep(t, Y1, r, get(X1, r) + out)))
        halo_start(t, PY)
        send_made(t, Y1)

        conv_local(t, PE, FT, 0)
        conv_local(t, PU, F, 1)
        conv_local(t, PY, G, 2)
        wgrad(t, PH, 1)
        for r in range(DH):
            widen(0, r, made[t, E1, :, pl.ds(r * W, W)].astype(f32))

        halo_arrived(t, PE)
        for r, out in conv_finish(t, PE, FT, 0):
            v = made[t, R2, :, pl.ds(r * W, W)].astype(f32)
            keep(t, E2, r, get(G2, r) + slope(v) * out)
        send_made(t, E2)
        halo_arrived(t, PU)
        if t == 1:
            wgrad(t, PU, 0)
        for r, out in conv_finish(t, PU, F, 1):
            keep(t, R1, r, get(O1, r) - out)
        send_made(t, R1)
        halo_arrived(t, PY)
        for r, out in conv_finish(t, PY, G, 2):
            keep(t, Y2, r, get(X2, r) + out)
        send_made(t, Y2)
        if t == 0:
            wgrad(t, PU, 0)

    tick(0, staged, lambda k: None)

    @pl.when(is_first)
    def _():
        for s in range(2):
            load_stage(X1 + s, nxt, s)
            for r in range(DH):
                second[X1 + s, :, pl.ds(r * W, W)] = staged(X1 + s, r).astype(bf16)

    @pl.when(is_last)
    def _():
        for s in range(2):
            last_grad(s).start()
            load_stage(G1 + s, loss, s)
            for r in range(DH):
                second[G1 + s, :, pl.ds(r * W, W)] = staged(G1 + s, r).astype(bf16)

    def arrived(k):
        if k <= X2:
            @pl.when(has_prev)
            def _():
                to_next(k).wait_recv()
        else:
            @pl.when(has_next)
            def _():
                to_prev(k).wait_recv()

    tick(1, lambda k, r: second[k, :, pl.ds(r * W, W)].astype(f32), arrived)

    for j in (1, 0):
        for q in range(1, n):
            share(j, q).wait_recv()
        total = dpart[j, slab]
        for q in range(1, n):
            total += dgot[j, q]
        dw[j] = total * scale

    for t in range(2):
        for k in range(6):
            halo_sent(t, k)
    for j in range(2):
        for q in range(1, n):
            share(j, q).wait_send()
    for k in (Y1, Y2):
        own_out(k).wait()

    @pl.when(is_last)
    def _():
        for k in (Y1, Y2):
            last_act(k).wait()
            last_grad(k).wait()

    @pl.when(has_next)
    def _():
        for k in (Y1, Y2):
            to_next(k).wait_send()
        for k in (R1, R2, E1, E2):
            out_prev(k).wait_recv()

    @pl.when(has_prev)
    def _():
        for k in (R1, R2, E1, E2):
            to_prev(k).wait_send()
            out_prev(k).wait_send()


def local(segs, n, fwd_in, back_out, back_grad, batch_next, loss_grad, weights):
    _, _, C, D, H, W = fwd_in.shape
    rows = C * D * H
    cs = C // n
    f32, bf16 = jnp.float32, jnp.bfloat16
    scale = float(D * n * H * W) ** (-0.5)
    kern = weights[0].reshape(2, C, C, 3, 3, 3)
    straight = kern.transpose(0, 3, 5, 1, 4, 2)
    turned = jnp.flip(kern, (3, 4, 5)).transpose(0, 3, 5, 2, 4, 1)
    w = jnp.concatenate([straight, turned], axis=0).reshape(4, 3, 3 * C, 3 * C)
    vmem = pl.BlockSpec(memory_space=pltpu.VMEM)
    anywhere = pl.BlockSpec(memory_space=pl.ANY)
    pair = jax.ShapeDtypeStruct((2, rows, W), bf16)
    dma = pltpu.SemaphoreType.DMA
    fout, backs, grads, dw = pl.pallas_call(
        functools.partial(kernel, (C, D, H, W, segs, n, scale)),
        out_shape=(pair, pair, pair, jax.ShapeDtypeStruct((2, 9, cs, 3 * C), f32)),
        in_specs=[vmem] * 6,
        out_specs=(anywhere, anywhere, anywhere, vmem),
        scratch_shapes=[
            pltpu.VMEM((2, 6, C, (D + 2) * (H + 2) * W), bf16),
            pltpu.VMEM((6, rows, W), f32),
            pltpu.VMEM((6, C, D * H * W), bf16),
            pltpu.VMEM((2, 6, C, D * H * W), bf16),
            pltpu.VMEM((6, rows, W), bf16),
            pltpu.VMEM((3, 3 * C, D * H * W), f32),
            pltpu.VMEM((2, 3 * C, D * H * W), bf16),
            pltpu.VMEM((2, 9 * C, 3 * C), f32),
            pltpu.VMEM((2, n, 9, cs, 3 * C), f32),
            pltpu.VMEM((2, n, 9, cs, 3 * C), f32),
            dma((2, 6, 2)),
            dma((2, 6, 2)),
            dma((2, 6)),
            dma((2, 6)),
            dma((6,)),
            dma((2, n)),
            dma((2, n)),
        ],
        compiler_params=pltpu.CompilerParams(
            collective_id=0, has_side_effects=True, vmem_limit_bytes=48 * 2**20
        ),
        name="petra",
    )(
        fwd_in.reshape(2, rows, W),
        back_out.reshape(2, rows, W),
        back_grad.reshape(2, rows, W),
        batch_next.reshape(2, rows, W),
        loss_grad.reshape(4, rows, W),
        w,
    )
    dw = dw.reshape(2, 3, 3, cs, 3, C).transpose(0, 5, 3, 1, 2, 4).reshape(1, 2, C, cs * 27)
    shape = fwd_in.shape
    return fout.reshape(shape), backs.reshape(shape), grads.reshape(shape), dw


def solution(mesh):
    field = P("segment", None, None, "slab", None, None)
    return jax.shard_map(
        functools.partial(local, mesh.shape["segment"], mesh.shape["slab"]),
        mesh=mesh,
        in_specs=(
            field,
            field,
            field,
            P(None, None, "slab", None, None),
            P(None, None, None, "slab", None, None),
            P("segment", None, None, None),
        ),
        out_specs=(field, field, field, P("segment", None, None, "slab")),
        check_vma=False,
    )
```

```python
import functools

import jax
import jax.numpy as jnp
from jax import lax
from jax.experimental import pallas as pl
from jax.experimental.pallas import tpu as pltpu
from jax.sharding import PartitionSpec as P

MESH = pl.DeviceIdType.MESH
F, G, FT, GT = range(4)
X1, X2, O1, O2, G1, G2 = range(6)
Y1, Y2, R1, R2, E1, E2 = range(6)
PX, PH, PD, PY, PU, PE = range(6)


def sigmoid(v):
    return 1.0 / (1.0 + jnp.exp(-v))


def silu(v):
    return v / (1.0 + jnp.exp(-v))


def slope(v):
    sig = sigmoid(v)
    return sig * (1.0 + v * (1.0 - sig))


def kernel(
    dims, fwd_hbm, bout_hbm, bgrad_hbm, nxt_hbm, loss_hbm, kern_hbm, fout, backs, grads, dw,
    fwd, bout, bgrad, nxt, loss, kern, kt, w, dt, pad, stage, second, made, nat, acc, g3, dsum, dpart, dgot,
    halo_s, halo_r, seg_s, seg_r, out_s, d_s, d_r, in_s,
):
    C, D, H, W, segs, n, scale = dims
    DH, HW = D * H, H * W
    cs = C // n
    LW = pl.cdiv(3 * C, 128) * 128
    f32, bf16 = jnp.float32, jnp.bfloat16
    seg = lax.axis_index("segment")
    slab = lax.axis_index("slab")
    has_prev, has_next = seg > 0, seg < segs - 1
    is_first, is_last = seg == 0, seg == segs - 1
    prev_seg = lax.rem(seg + segs - 1, segs)
    next_seg = lax.rem(seg + 1, segs)
    lane_no = lax.broadcasted_iota(jnp.int32, (C, W), 1)

    fetches = [
        pltpu.make_async_copy(src, dst, in_s.at[i])
        for i, (src, dst) in enumerate(
            [
                (bgrad_hbm, bgrad), (bout_hbm, bout), (fwd_hbm, fwd),
                (kern_hbm, kern), (nxt_hbm, nxt), (loss_hbm, loss),
            ]
        )
    ]
    for fetch in fetches:
        fetch.start()

    barrier = pltpu.get_barrier_semaphore()

    @pl.when(has_prev)
    def _():
        pl.semaphore_signal(barrier, inc=1, device_id={"segment": prev_seg}, device_id_type=MESH)

    @pl.when(has_next)
    def _():
        pl.semaphore_signal(barrier, inc=1, device_id={"segment": next_seg}, device_id_type=MESH)

    for k in range(1, n):
        pl.semaphore_signal(
            barrier, inc=1, device_id={"slab": lax.rem(slab + k, n)}, device_id_type=MESH
        )

    def lane(q, hh):
        return (q * (H + 2) + hh) * W

    zero = jnp.zeros((C, W), bf16)
    for t in range(2):
        for k in range(6):
            for q in range(D + 2):
                for hh in (0, H + 1):
                    pad[t, k, :, pl.ds(lane(q, hh), W)] = zero

    @pl.when(slab == 0)
    def _():
        for t in range(2):
            for k in range(6):
                pad[t, k, :, pl.ds(lane(0, 1), HW)] = jnp.zeros((C, HW), bf16)

    @pl.when(slab == n - 1)
    def _():
        for t in range(2):
            for k in range(6):
                pad[t, k, :, pl.ds(lane(D + 1, 1), HW)] = jnp.zeros((C, HW), bf16)

    def load_stage(slot, ref, s):
        stage[slot] = ref[s].astype(f32)

    def staged(slot, r):
        return stage[slot, pl.ds(r, C, stride=DH), :]

    def prepare_weights():
        fetches[3].wait()
        wide = kern[...].astype(f32)
        kt[...] = jnp.concatenate([wide, jnp.zeros((LW - 2 * C, 27 * C), f32)], axis=0).T

        def tap(t):
            return kt[pl.ds(t, C, stride=27), :]

        for a in range(3):
            for c in range(3):
                block = jnp.concatenate([tap(9 * a + 3 * b + c) for b in range(3)], axis=0).T
                for f in range(2):
                    w[F + f, a, c * C : (c + 1) * C, :] = block[f * C : (f + 1) * C].astype(bf16)
                for f in range(2):
                    turned = jnp.concatenate(
                        [
                            tap(9 * (2 - a) + 3 * (2 - b) + 2 - c)[:, f * C : (f + 1) * C]
                            for b in range(3)
                        ],
                        axis=1,
                    )
                    w[FT + f, a, c * C : (c + 1) * C, :] = turned.astype(bf16)

    def load_pair(i, slot, ref):
        fetches[i].wait()
        for s in range(2):
            load_stage(slot + s, ref, s)

    def halo(t, k, up):
        src_q, dst_q = (D, 0) if up else (1, D + 1)
        target = lax.rem(slab + (1 if up else n - 1), n)
        return pltpu.make_async_remote_copy(
            src_ref=pad.at[t, k, :, pl.ds(lane(src_q, 1), HW)],
            dst_ref=pad.at[t, k, :, pl.ds(lane(dst_q, 1), HW)],
            send_sem=halo_s.at[t, k, up],
            recv_sem=halo_r.at[t, k, up],
            device_id={"slab": target},
            device_id_type=MESH,
        )

    def halo_start(t, k):
        @pl.when(slab < n - 1)
        def _():
            halo(t, k, 1).start()

        @pl.when(slab > 0)
        def _():
            halo(t, k, 0).start()

    def halo_arrived(t, k):
        @pl.when(slab > 0)
        def _():
            halo(t, k, 1).wait_recv()

        @pl.when(slab < n - 1)
        def _():
            halo(t, k, 0).wait_recv()

    def halo_sent(t, k):
        @pl.when(slab < n - 1)
        def _():
            halo(t, k, 1).wait_send()

        @pl.when(slab > 0)
        def _():
            halo(t, k, 0).wait_send()

    def to_next(k):
        return pltpu.make_async_remote_copy(
            src_ref=made.at[0, k], dst_ref=second.at[X1 + k],
            send_sem=seg_s.at[0, k], recv_sem=seg_r.at[0, k],
            device_id={"segment": next_seg}, device_id_type=MESH,
        )

    def to_prev(k):
        return pltpu.make_async_remote_copy(
            src_ref=made.at[0, k], dst_ref=second.at[k],
            send_sem=seg_s.at[0, k], recv_sem=seg_r.at[0, k],
            device_id={"segment": prev_seg}, device_id_type=MESH,
        )

    def out_prev(k):
        dst = backs.at[k - R1] if k < E1 else grads.at[k - E1]
        return pltpu.make_async_remote_copy(
            src_ref=nat.at[k], dst_ref=dst,
            send_sem=seg_s.at[1, k], recv_sem=seg_r.at[1, k],
            device_id={"segment": prev_seg}, device_id_type=MESH,
        )

    def own_out(k):
        return pltpu.make_async_copy(nat.at[k], fout.at[k], out_s.at[k])

    def last_act(k):
        return pltpu.make_async_copy(nat.at[k], backs.at[k], out_s.at[2 + k])

    def last_grad(k):
        return pltpu.make_async_copy(loss.at[2 + k], grads.at[k], out_s.at[4 + k])

    def put(t, k, r, value):
        d, h = divmod(r, H)
        pad[t, k, :, pl.ds(lane(d + 1, h + 1), W)] = value.astype(bf16)

    def tall(t, k, q):
        return jnp.concatenate([pad[t, k, :, pl.ds(lane(q, b), HW)] for b in range(3)], axis=0)

    def conv_local(t, k, m, slot):
        for p in range(D):
            total = None
            for a in range(3):
                if 1 <= p + a <= D:
                    part = jnp.dot(w[m, a], tall(t, k, p + a), preferred_element_type=f32)
                    total = part if total is None else total + part
            acc[slot, :, pl.ds(p * HW, HW)] = total

    def conv_finish(t, k, m, slot):
        for p in range(D):
            total = acc[slot, :, pl.ds(p * HW, HW)]
            for a in range(3):
                if not 1 <= p + a <= D:
                    total += jnp.dot(w[m, a], tall(t, k, p + a), preferred_element_type=f32)
            for h in range(H):
                y = total[:, h * W : (h + 1) * W]
                left = jnp.where(lane_no == 0, 0.0, pltpu.roll(y[:C], 1, 1))
                right = jnp.where(lane_no == W - 1, 0.0, pltpu.roll(y[2 * C :], W - 1, 1))
                yield p * H + h, y[C : 2 * C] + left + right

    def widen(j, r, v):
        at = pl.ds(r * W, W)
        g3[j, 0:C, at] = jnp.where(lane_no == W - 1, 0.0, pltpu.roll(v, W - 1, 1)).astype(bf16)
        g3[j, C : 2 * C, at] = v.astype(bf16)
        g3[j, 2 * C : 3 * C, at] = jnp.where(lane_no == 0, 0.0, pltpu.roll(v, 1, 1)).astype(bf16)

    def wgrad(t, k, j):
        total = None
        for p in range(D):
            lhs = jnp.concatenate([tall(t, k, p + a) for a in range(3)], axis=0)
            part = lax.dot_general(
                lhs, g3[j, :, pl.ds(p * HW, HW)], (((1,), (1,)), ((), ())),
                preferred_element_type=f32,
            )
            total = part if total is None else total + part
        if t == 0:
            dsum[j] = total
            return
        total += dsum[j]
        total = jnp.concatenate([total, jnp.zeros((9 * C, LW - 3 * C), f32)], axis=1)
        for q in range(n):
            for ab in range(9):
                dpart[j, q, ab] = total[ab * C + q * cs : ab * C + (q + 1) * cs]
        for q in range(1, n):
            share(j, q).start()

    def share(j, q):
        target = lax.rem(slab + q, n)
        return pltpu.make_async_remote_copy(
            src_ref=dpart.at[j, target], dst_ref=dgot.at[j, q],
            send_sem=d_s.at[j, q], recv_sem=d_r.at[j, q],
            device_id={"slab": target}, device_id_type=MESH,
        )

    def keep(t, k, r, value):
        held = value.astype(bf16)
        made[t, k, :, pl.ds(r * W, W)] = held
        wide = held.astype(f32)
        if t == 1:
            stage[k, pl.ds(r, C, stride=DH), :] = wide
        return wide

    def send_made(t, k):
        if t == 0:
            if k < R1:
                @pl.when(has_next)
                def _():
                    to_next(k).start()

                @pl.when(is_last)
                def _():
                    second[O1 + k] = made[0, k]
            else:
                @pl.when(has_prev)
                def _():
                    to_prev(k).start()
            return
        nat[k] = stage[k].astype(bf16)
        if k < R1:
            own_out(k).start()

            @pl.when(is_last)
            def _():
                last_act(k).start()
        else:
            @pl.when(has_prev)
            def _():
                out_prev(k).start()

    def tick(t, get, ready):
        if t == 0:
            load_pair(0, G1, bgrad)
        ready(G2)
        for r in range(DH):
            put(t, PD, r, get(G2, r))
        if t == 0:
            peers = has_prev.astype(jnp.int32) + has_next.astype(jnp.int32) + n - 1
            pl.semaphore_wait(barrier, peers)
        halo_start(t, PD)
        if t == 0:
            load_pair(1, O1, bout)
        ready(O1)
        for r in range(DH):
            put(t, PH, r, silu(get(O1, r)))
        halo_start(t, PH)
        if t == 0:
            load_pair(2, X1, fwd)
        ready(X2)
        for r in range(DH):
            put(t, PX, r, silu(get(X2, r)))
        halo_start(t, PX)
        if t == 0:
            prepare_weights()
        conv_local(t, PD, GT, 0)
        conv_local(t, PH, G, 1)
        conv_local(t, PX, F, 2)
        for r in range(DH):
            widen(1, r, get(G2, r))

        ready(G1)
        halo_arrived(t, PD)
        for r, out in conv_finish(t, PD, GT, 0):
            put(t, PE, r, keep(t, E1, r, get(G1, r) + slope(get(O1, r)) * out))
        halo_start(t, PE)
        send_made(t, E1)
        ready(O2)
        halo_arrived(t, PH)
        for r, out in conv_finish(t, PH, G, 1):
            put(t, PU, r, silu(keep(t, R2, r, get(O2, r) - out)))
        halo_start(t, PU)
        send_made(t, R2)
        ready(X1)
        halo_arrived(t, PX)
        for r, out in conv_finish(t, PX, F, 2):
            put(t, PY, r, silu(keep(t, Y1, r, get(X1, r) + out)))
        halo_start(t, PY)
        send_made(t, Y1)

        conv_local(t, PE, FT, 0)
        conv_local(t, PU, F, 1)
        conv_local(t, PY, G, 2)
        wgrad(t, PH, 1)
        for r in range(DH):
            widen(0, r, made[t, E1, :, pl.ds(r * W, W)].astype(f32))

        halo_arrived(t, PE)
        for r, out in conv_finish(t, PE, FT, 0):
            v = made[t, R2, :, pl.ds(r * W, W)].astype(f32)
            keep(t, E2, r, get(G2, r) + slope(v) * out)
        send_made(t, E2)
        halo_arrived(t, PU)
        if t == 1:
            wgrad(t, PU, 0)
        for r, out in conv_finish(t, PU, F, 1):
            keep(t, R1, r, get(O1, r) - out)
        send_made(t, R1)
        halo_arrived(t, PY)
        for r, out in conv_finish(t, PY, G, 2):
            keep(t, Y2, r, get(X2, r) + out)
        send_made(t, Y2)
        if t == 0:
            wgrad(t, PU, 0)

    tick(0, staged, lambda k: None)

    fetches[4].wait()
    fetches[5].wait()

    @pl.when(is_first)
    def _():
        for s in range(2):
            load_stage(X1 + s, nxt, s)
            for r in range(DH):
                second[X1 + s, :, pl.ds(r * W, W)] = staged(X1 + s, r).astype(bf16)

    @pl.when(is_last)
    def _():
        for s in range(2):
            last_grad(s).start()
            load_stage(G1 + s, loss, s)
            for r in range(DH):
                second[G1 + s, :, pl.ds(r * W, W)] = staged(G1 + s, r).astype(bf16)

    def arrived(k):
        if k <= X2:
            @pl.when(has_prev)
            def _():
                to_next(k).wait_recv()
        else:
            @pl.when(has_next)
            def _():
                to_prev(k).wait_recv()

    tick(1, lambda k, r: second[k, :, pl.ds(r * W, W)].astype(f32), arrived)

    for j in (1, 0):
        for q in range(1, n):
            share(j, q).wait_recv()
        total = dpart[j, slab]
        for q in range(1, n):
            total += dgot[j, q]
        total *= scale
        for ab in range(9):
            for c in range(3):
                tap = total[ab] if c == 0 else pltpu.roll(total[ab], LW - c * C, 1)
                dt[j, pl.ds(3 * ab + c, cs, stride=27), :] = tap
        dw[j] = dt[j].T[:C]

    for t in range(2):
        for k in range(6):
            halo_sent(t, k)
    for j in range(2):
        for q in range(1, n):
            share(j, q).wait_send()
    for k in (Y1, Y2):
        own_out(k).wait()

    @pl.when(is_last)
    def _():
        for k in (Y1, Y2):
            last_act(k).wait()
            last_grad(k).wait()

    @pl.when(has_next)
    def _():
        for k in (Y1, Y2):
            to_next(k).wait_send()
        for k in (R1, R2, E1, E2):
            out_prev(k).wait_recv()

    @pl.when(has_prev)
    def _():
        for k in (R1, R2, E1, E2):
            to_prev(k).wait_send()
            out_prev(k).wait_send()


def write_out(*refs):
    srcs, dsts, tiles, sems = refs[:4], refs[4:8], refs[8:12], refs[12]
    reads = [pltpu.make_async_copy(a, b, sems.at[0, i]) for i, (a, b) in enumerate(zip(srcs, tiles))]
    writes = [pltpu.make_async_copy(a, b, sems.at[1, i]) for i, (a, b) in enumerate(zip(tiles, dsts))]
    for read in reads:
        read.start()
    for read, write in zip(reads, writes):
        read.wait()
        write.start()
    for write in writes:
        write.wait()


def local(segs, n, fwd_in, back_out, back_grad, batch_next, loss_grad, weights):
    _, _, C, D, H, W = fwd_in.shape
    rows = C * D * H
    cs = C // n
    f32, bf16 = jnp.float32, jnp.bfloat16
    scale = float(D * n * H * W) ** (-0.5)
    vmem = pl.BlockSpec(memory_space=pltpu.VMEM)
    hbm = pl.BlockSpec(memory_space=pltpu.HBM)
    wide = pl.cdiv(3 * C, 128) * 128
    anywhere = pl.BlockSpec(memory_space=pl.ANY)
    pair = jax.ShapeDtypeStruct((2, rows, W), bf16)
    share = jax.ShapeDtypeStruct((2, C, 27 * cs), f32)
    dma = pltpu.SemaphoreType.DMA
    fout, backs, grads, dw = pl.pallas_call(
        functools.partial(kernel, (C, D, H, W, segs, n, scale)),
        out_shape=(pair, pair, pair, share),
        in_specs=[hbm] * 6,
        out_specs=(anywhere, anywhere, anywhere, vmem),
        scratch_shapes=[
            pltpu.VMEM((2, rows, W), bf16),
            pltpu.VMEM((2, rows, W), bf16),
            pltpu.VMEM((2, rows, W), bf16),
            pltpu.VMEM((2, rows, W), bf16),
            pltpu.VMEM((4, rows, W), bf16),
            pltpu.VMEM((2 * C, 27 * C), bf16),
            pltpu.VMEM((27 * C, wide), f32),
            pltpu.VMEM((4, 3, 3 * C, 3 * C), bf16),
            pltpu.VMEM((2, 27 * cs, wide), f32),
            pltpu.VMEM((2, 6, C, (D + 2) * (H + 2) * W), bf16),
            pltpu.VMEM((6, rows, W), f32),
            pltpu.VMEM((6, C, D * H * W), bf16),
            pltpu.VMEM((2, 6, C, D * H * W), bf16),
            pltpu.VMEM((6, rows, W), bf16),
            pltpu.VMEM((3, 3 * C, D * H * W), f32),
            pltpu.VMEM((2, 3 * C, D * H * W), bf16),
            pltpu.VMEM((2, 9 * C, 3 * C), f32),
            pltpu.VMEM((2, n, 9, cs, wide), f32),
            pltpu.VMEM((2, n, 9, cs, wide), f32),
            dma((2, 6, 2)),
            dma((2, 6, 2)),
            dma((2, 6)),
            dma((2, 6)),
            dma((6,)),
            dma((2, n)),
            dma((2, n)),
            dma((6,)),
        ],
        compiler_params=pltpu.CompilerParams(
            collective_id=0, has_side_effects=True, vmem_limit_bytes=67043328
        ),
        name="petra",
    )(
        fwd_in.reshape(2, rows, W),
        back_out.reshape(2, rows, W),
        back_grad.reshape(2, rows, W),
        batch_next.reshape(2, rows, W),
        loss_grad.reshape(4, rows, W),
        weights.reshape(2 * C, 27 * C),
    )
    fout, backs, grads, dw = pl.pallas_call(
        write_out,
        out_shape=(pair, pair, pair, share),
        in_specs=[hbm] * 4,
        out_specs=(hbm,) * 4,
        scratch_shapes=[pltpu.VMEM(x.shape, x.dtype) for x in (pair, pair, pair, share)]
        + [dma((2, 4))],
        compiler_params=pltpu.CompilerParams(vmem_limit_bytes=67043328),
        name="write_out",
    )(fout, backs, grads, dw)
    shape = fwd_in.shape
    return fout.reshape(shape), backs.reshape(shape), grads.reshape(shape), dw[None]


def solution(mesh):
    field = P("segment", None, None, "slab", None, None)
    return jax.shard_map(
        functools.partial(local, mesh.shape["segment"], mesh.shape["slab"]),
        mesh=mesh,
        in_specs=(
            field,
            field,
            field,
            P(None, None, "slab", None, None),
            P(None, None, None, "slab", None, None),
            P("segment", None, None, None),
        ),
        out_specs=(field, field, field, P("segment", None, None, "slab")),
        check_vma=False,
    )
```

```python
import functools

import jax
import jax.numpy as jnp
from jax import lax
from jax.experimental import pallas as pl
from jax.experimental.pallas import tpu as pltpu
from jax.sharding import PartitionSpec as P

MESH = pl.DeviceIdType.MESH
F, G, FT, GT = range(4)
X1, X2, O1, O2, G1, G2 = range(6)
Y1, Y2, R1, R2, E1, E2 = range(6)
PX, PH, PD, PY, PU, PE = range(6)


def sigmoid(v):
    return 1.0 / (1.0 + jnp.exp(-v))


def silu(v):
    return v / (1.0 + jnp.exp(-v))


def slope(v):
    sig = sigmoid(v)
    return sig * (1.0 + v * (1.0 - sig))


def kernel(
    dims, fwd_hbm, bout_hbm, bgrad_hbm, nxt_hbm, loss_hbm, kern_hbm, fout, backs, grads, dw,
    fwd, bout, bgrad, nxt, loss, kern, kt, w, dt, pad, stage, second, made, nat, acc, g3, dsum, dpart, dgot,
    halo_s, halo_r, seg_s, seg_r, out_s, d_s, d_r, in_s, edge, diag_s,
):
    C, D, H, W, segs, n, scale = dims
    DH, HW = D * H, H * W
    cs = C // n
    LW = pl.cdiv(3 * C, 128) * 128
    f32, bf16 = jnp.float32, jnp.bfloat16
    seg = lax.axis_index("segment")
    slab = lax.axis_index("slab")
    has_prev, has_next = seg > 0, seg < segs - 1
    is_first, is_last = seg == 0, seg == segs - 1
    prev_seg = lax.rem(seg + segs - 1, segs)
    next_seg = lax.rem(seg + 1, segs)
    lane_no = lax.broadcasted_iota(jnp.int32, (C, W), 1)

    fetches = [
        pltpu.make_async_copy(src, dst, in_s.at[i])
        for i, (src, dst) in enumerate(
            [
                (bgrad_hbm, bgrad), (bout_hbm, bout), (fwd_hbm, fwd),
                (kern_hbm, kern), (nxt_hbm, nxt), (loss_hbm, loss),
            ]
        )
    ]
    for fetch in fetches:
        fetch.start()

    barrier = pltpu.get_barrier_semaphore()

    up_slab, down_slab = lax.rem(slab + 1, n), lax.rem(slab + n - 1, n)
    has_up, has_down = slab < n - 1, slab > 0

    for there, target in ((has_prev, prev_seg), (has_next, next_seg)):
        @pl.when(there)
        def _():
            pl.semaphore_signal(
                barrier, inc=1, device_id={"segment": target}, device_id_type=MESH
            )

        for side, beside in ((has_up, up_slab), (has_down, down_slab)):
            @pl.when(there & side)
            def _():
                pl.semaphore_signal(
                    barrier, inc=1, device_id={"segment": target, "slab": beside},
                    device_id_type=MESH,
                )

    for k in range(1, n):
        pl.semaphore_signal(
            barrier, inc=1, device_id={"slab": lax.rem(slab + k, n)}, device_id_type=MESH
        )

    def lane(q, hh):
        return (q * (H + 2) + hh) * W

    zero = jnp.zeros((C, W), bf16)
    for t in range(2):
        for k in range(6):
            for q in range(D + 2):
                for hh in (0, H + 1):
                    pad[t, k, :, pl.ds(lane(q, hh), W)] = zero

    @pl.when(slab == 0)
    def _():
        for t in range(2):
            for k in range(6):
                pad[t, k, :, pl.ds(lane(0, 1), HW)] = jnp.zeros((C, HW), bf16)

    @pl.when(slab == n - 1)
    def _():
        for t in range(2):
            for k in range(6):
                pad[t, k, :, pl.ds(lane(D + 1, 1), HW)] = jnp.zeros((C, HW), bf16)

    def load_stage(slot, ref, s):
        stage[slot] = ref[s].astype(f32)

    def staged(slot, r):
        return stage[slot, pl.ds(r, C, stride=DH), :]

    def prepare_weights():
        fetches[3].wait()
        wide = kern[...].astype(f32)
        kt[...] = jnp.concatenate([wide, jnp.zeros((LW - 2 * C, 27 * C), f32)], axis=0).T

        def tap(t):
            return kt[pl.ds(t, C, stride=27), :]

        for a in range(3):
            for c in range(3):
                block = jnp.concatenate([tap(9 * a + 3 * b + c) for b in range(3)], axis=0).T
                for f in range(2):
                    w[F + f, a, c * C : (c + 1) * C, :] = block[f * C : (f + 1) * C].astype(bf16)
                for f in range(2):
                    turned = jnp.concatenate(
                        [
                            tap(9 * (2 - a) + 3 * (2 - b) + 2 - c)[:, f * C : (f + 1) * C]
                            for b in range(3)
                        ],
                        axis=1,
                    )
                    w[FT + f, a, c * C : (c + 1) * C, :] = turned.astype(bf16)

    def load_pair(i, slot, ref):
        fetches[i].wait()
        for s in range(2):
            load_stage(slot + s, ref, s)

    def halo(t, k, up):
        src_q, dst_q = (D, 0) if up else (1, D + 1)
        target = lax.rem(slab + (1 if up else n - 1), n)
        return pltpu.make_async_remote_copy(
            src_ref=pad.at[t, k, :, pl.ds(lane(src_q, 1), HW)],
            dst_ref=pad.at[t, k, :, pl.ds(lane(dst_q, 1), HW)],
            send_sem=halo_s.at[t, k, up],
            recv_sem=halo_r.at[t, k, up],
            device_id={"slab": target},
            device_id_type=MESH,
        )

    def exchanged(t, k):
        if t == 0 or k >= PY:
            return seg >= 0
        return is_first if k == PX else is_last

    def halo_start(t, k):
        @pl.when(exchanged(t, k) & has_up)
        def _():
            halo(t, k, 1).start()

        @pl.when(exchanged(t, k) & has_down)
        def _():
            halo(t, k, 0).start()

    def diagonal(k, up):
        src = made.at[0, E2] if k == PD else edge.at[0 if k == PH else 1]
        plane, dst_q = (D - 1, 0) if up else (0, D + 1)
        return pltpu.make_async_remote_copy(
            src_ref=src.at[:, pl.ds(plane * HW, HW)],
            dst_ref=pad.at[1, k, :, pl.ds(lane(dst_q, 1), HW)],
            send_sem=diag_s.at[k, up],
            recv_sem=halo_r.at[1, k, up],
            device_id={
                "segment": next_seg if k == PX else prev_seg,
                "slab": up_slab if up else down_slab,
            },
            device_id_type=MESH,
        )

    def each_diagonal(k, act):
        there = has_next if k == PX else has_prev
        for up, side in ((1, has_up), (0, has_down)):
            @pl.when(there & side)
            def _():
                act(diagonal(k, up))

    def halo_arrived(t, k):
        @pl.when(slab > 0)
        def _():
            halo(t, k, 1).wait_recv()

        @pl.when(slab < n - 1)
        def _():
            halo(t, k, 0).wait_recv()

    def halo_sent(t, k):
        @pl.when(exchanged(t, k) & has_up)
        def _():
            halo(t, k, 1).wait_send()

        @pl.when(exchanged(t, k) & has_down)
        def _():
            halo(t, k, 0).wait_send()

    def to_next(k):
        return pltpu.make_async_remote_copy(
            src_ref=made.at[0, k], dst_ref=second.at[X1 + k],
            send_sem=seg_s.at[0, k], recv_sem=seg_r.at[0, k],
            device_id={"segment": next_seg}, device_id_type=MESH,
        )

    def to_prev(k):
        return pltpu.make_async_remote_copy(
            src_ref=made.at[0, k], dst_ref=second.at[k],
            send_sem=seg_s.at[0, k], recv_sem=seg_r.at[0, k],
            device_id={"segment": prev_seg}, device_id_type=MESH,
        )

    def out_prev(k):
        dst = backs.at[k - R1] if k < E1 else grads.at[k - E1]
        return pltpu.make_async_remote_copy(
            src_ref=nat.at[k], dst_ref=dst,
            send_sem=seg_s.at[1, k], recv_sem=seg_r.at[1, k],
            device_id={"segment": prev_seg}, device_id_type=MESH,
        )

    def own_out(k):
        return pltpu.make_async_copy(nat.at[k], fout.at[k], out_s.at[k])

    def last_act(k):
        return pltpu.make_async_copy(nat.at[k], backs.at[k], out_s.at[2 + k])

    def last_grad(k):
        return pltpu.make_async_copy(loss.at[2 + k], grads.at[k], out_s.at[4 + k])

    def put(t, k, r, value):
        d, h = divmod(r, H)
        pad[t, k, :, pl.ds(lane(d + 1, h + 1), W)] = value.astype(bf16)

    def tall(t, k, q):
        return jnp.concatenate([pad[t, k, :, pl.ds(lane(q, b), HW)] for b in range(3)], axis=0)

    def conv_local(t, k, m, slot):
        for p in range(D):
            total = None
            for a in range(3):
                if 1 <= p + a <= D:
                    part = jnp.dot(w[m, a], tall(t, k, p + a), preferred_element_type=f32)
                    total = part if total is None else total + part
            acc[slot, :, pl.ds(p * HW, HW)] = total

    def conv_finish(t, k, m, slot):
        for p in range(D):
            total = acc[slot, :, pl.ds(p * HW, HW)]
            for a in range(3):
                if not 1 <= p + a <= D:
                    total += jnp.dot(w[m, a], tall(t, k, p + a), preferred_element_type=f32)
            for h in range(H):
                y = total[:, h * W : (h + 1) * W]
                left = jnp.where(lane_no == 0, 0.0, pltpu.roll(y[:C], 1, 1))
                right = jnp.where(lane_no == W - 1, 0.0, pltpu.roll(y[2 * C :], W - 1, 1))
                yield p * H + h, y[C : 2 * C] + left + right

    def widen(j, r, v):
        at = pl.ds(r * W, W)
        g3[j, 0:C, at] = jnp.where(lane_no == W - 1, 0.0, pltpu.roll(v, W - 1, 1)).astype(bf16)
        g3[j, C : 2 * C, at] = v.astype(bf16)
        g3[j, 2 * C : 3 * C, at] = jnp.where(lane_no == 0, 0.0, pltpu.roll(v, 1, 1)).astype(bf16)

    def wgrad(t, k, j):
        total = None
        for p in range(D):
            lhs = jnp.concatenate([tall(t, k, p + a) for a in range(3)], axis=0)
            part = lax.dot_general(
                lhs, g3[j, :, pl.ds(p * HW, HW)], (((1,), (1,)), ((), ())),
                preferred_element_type=f32,
            )
            total = part if total is None else total + part
        if t == 0:
            dsum[j] = total
            return
        total += dsum[j]
        total = jnp.concatenate([total, jnp.zeros((9 * C, LW - 3 * C), f32)], axis=1)
        for q in range(n):
            for ab in range(9):
                dpart[j, q, ab] = total[ab * C + q * cs : ab * C + (q + 1) * cs]
        for q in range(1, n):
            share(j, q).start()

    def share(j, q):
        target = lax.rem(slab + q, n)
        return pltpu.make_async_remote_copy(
            src_ref=dpart.at[j, target], dst_ref=dgot.at[j, q],
            send_sem=d_s.at[j, q], recv_sem=d_r.at[j, q],
            device_id={"slab": target}, device_id_type=MESH,
        )

    def keep(t, k, r, value):
        held = value.astype(bf16)
        made[t, k, :, pl.ds(r * W, W)] = held
        wide = held.astype(f32)
        if t == 1:
            stage[k, pl.ds(r, C, stride=DH), :] = wide
        return wide

    def send_made(t, k):
        if t == 0:
            if k < R1:
                @pl.when(has_next)
                def _():
                    to_next(k).start()

                @pl.when(is_last)
                def _():
                    second[O1 + k] = made[0, k]
            else:
                @pl.when(has_prev)
                def _():
                    to_prev(k).start()
            return
        nat[k] = stage[k].astype(bf16)
        if k < R1:
            own_out(k).start()

            @pl.when(is_last)
            def _():
                last_act(k).start()
        else:
            @pl.when(has_prev)
            def _():
                out_prev(k).start()

    def tick(t, get, ready):
        if t == 0:
            load_pair(0, G1, bgrad)
        ready(G2)
        for r in range(DH):
            put(t, PD, r, get(G2, r))
        if t == 0:
            ends = has_prev.astype(jnp.int32) + has_next.astype(jnp.int32)
            sides = has_up.astype(jnp.int32) + has_down.astype(jnp.int32)
            peers = ends * (1 + sides) + n - 1
            pl.semaphore_wait(barrier, peers)
        halo_start(t, PD)
        if t == 0:
            load_pair(1, O1, bout)
        ready(O1)
        for r in range(DH):
            put(t, PH, r, silu(get(O1, r)))
        halo_start(t, PH)
        if t == 0:
            load_pair(2, X1, fwd)
        ready(X2)
        for r in range(DH):
            put(t, PX, r, silu(get(X2, r)))
        halo_start(t, PX)
        if t == 0:
            prepare_weights()
        conv_local(t, PD, GT, 0)
        conv_local(t, PH, G, 1)
        conv_local(t, PX, F, 2)
        for r in range(DH):
            widen(1, r, get(G2, r))

        ready(G1)
        halo_arrived(t, PD)
        for r, out in conv_finish(t, PD, GT, 0):
            put(t, PE, r, keep(t, E1, r, get(G1, r) + slope(get(O1, r)) * out))
        halo_start(t, PE)
        send_made(t, E1)
        ready(O2)
        halo_arrived(t, PH)
        for r, out in conv_finish(t, PH, G, 1):
            put(t, PU, r, silu(keep(t, R2, r, get(O2, r) - out)))
        halo_start(t, PU)
        send_made(t, R2)
        ready(X1)
        halo_arrived(t, PX)
        for r, out in conv_finish(t, PX, F, 2):
            put(t, PY, r, silu(keep(t, Y1, r, get(X1, r) + out)))
        halo_start(t, PY)
        send_made(t, Y1)

        conv_local(t, PE, FT, 0)
        conv_local(t, PU, F, 1)
        conv_local(t, PY, G, 2)
        wgrad(t, PH, 1)
        for r in range(DH):
            widen(0, r, made[t, E1, :, pl.ds(r * W, W)].astype(f32))

        halo_arrived(t, PE)
        for r, out in conv_finish(t, PE, FT, 0):
            v = made[t, R2, :, pl.ds(r * W, W)].astype(f32)
            keep(t, E2, r, get(G2, r) + slope(v) * out)
        if t == 0:
            each_diagonal(PD, lambda copy: copy.start())
        send_made(t, E2)
        halo_arrived(t, PU)
        if t == 1:
            wgrad(t, PU, 0)
        for r, out in conv_finish(t, PU, F, 1):
            wide = keep(t, R1, r, get(O1, r) - out)
            if t == 0:
                edge[0, :, pl.ds(r * W, W)] = silu(wide).astype(bf16)
        if t == 0:
            each_diagonal(PH, lambda copy: copy.start())
        send_made(t, R1)
        halo_arrived(t, PY)
        for r, out in conv_finish(t, PY, G, 2):
            wide = keep(t, Y2, r, get(X2, r) + out)
            if t == 0:
                edge[1, :, pl.ds(r * W, W)] = silu(wide).astype(bf16)
        if t == 0:
            each_diagonal(PX, lambda copy: copy.start())
        send_made(t, Y2)
        if t == 0:
            wgrad(t, PU, 0)

    tick(0, staged, lambda k: None)

    fetches[4].wait()
    fetches[5].wait()

    @pl.when(is_first)
    def _():
        for s in range(2):
            load_stage(X1 + s, nxt, s)
            for r in range(DH):
                second[X1 + s, :, pl.ds(r * W, W)] = staged(X1 + s, r).astype(bf16)

    @pl.when(is_last)
    def _():
        for s in range(2):
            last_grad(s).start()
            load_stage(G1 + s, loss, s)
            for r in range(DH):
                second[G1 + s, :, pl.ds(r * W, W)] = staged(G1 + s, r).astype(bf16)

    def arrived(k):
        if k <= X2:
            @pl.when(has_prev)
            def _():
                to_next(k).wait_recv()
        else:
            @pl.when(has_next)
            def _():
                to_prev(k).wait_recv()

    tick(1, lambda k, r: second[k, :, pl.ds(r * W, W)].astype(f32), arrived)

    for j in (1, 0):
        for q in range(1, n):
            share(j, q).wait_recv()
        total = dpart[j, slab]
        for q in range(1, n):
            total += dgot[j, q]
        total *= scale
        for ab in range(9):
            for c in range(3):
                tap = total[ab] if c == 0 else pltpu.roll(total[ab], LW - c * C, 1)
                dt[j, pl.ds(3 * ab + c, cs, stride=27), :] = tap
        dw[j] = dt[j].T[:C]

    for t in range(2):
        for k in range(6):
            halo_sent(t, k)
    for k in (PD, PH, PX):
        each_diagonal(k, lambda copy: copy.wait_send())
    for j in range(2):
        for q in range(1, n):
            share(j, q).wait_send()
    for k in (Y1, Y2):
        own_out(k).wait()

    @pl.when(is_last)
    def _():
        for k in (Y1, Y2):
            last_act(k).wait()
            last_grad(k).wait()

    @pl.when(has_next)
    def _():
        for k in (Y1, Y2):
            to_next(k).wait_send()
        for k in (R1, R2, E1, E2):
            out_prev(k).wait_recv()

    @pl.when(has_prev)
    def _():
        for k in (R1, R2, E1, E2):
            to_prev(k).wait_send()
            out_prev(k).wait_send()


def write_out(*refs):
    srcs, dsts, tiles, sems = refs[:4], refs[4:8], refs[8:12], refs[12]
    reads = [pltpu.make_async_copy(a, b, sems.at[0, i]) for i, (a, b) in enumerate(zip(srcs, tiles))]
    writes = [pltpu.make_async_copy(a, b, sems.at[1, i]) for i, (a, b) in enumerate(zip(tiles, dsts))]
    for read in reads:
        read.start()
    for read, write in zip(reads, writes):
        read.wait()
        write.start()
    for write in writes:
        write.wait()


def local(segs, n, fwd_in, back_out, back_grad, batch_next, loss_grad, weights):
    _, _, C, D, H, W = fwd_in.shape
    rows = C * D * H
    cs = C // n
    f32, bf16 = jnp.float32, jnp.bfloat16
    scale = float(D * n * H * W) ** (-0.5)
    vmem = pl.BlockSpec(memory_space=pltpu.VMEM)
    hbm = pl.BlockSpec(memory_space=pltpu.HBM)
    wide = pl.cdiv(3 * C, 128) * 128
    anywhere = pl.BlockSpec(memory_space=pl.ANY)
    pair = jax.ShapeDtypeStruct((2, rows, W), bf16)
    share = jax.ShapeDtypeStruct((2, C, 27 * cs), f32)
    dma = pltpu.SemaphoreType.DMA
    fout, backs, grads, dw = pl.pallas_call(
        functools.partial(kernel, (C, D, H, W, segs, n, scale)),
        out_shape=(pair, pair, pair, share),
        in_specs=[hbm] * 6,
        out_specs=(anywhere, anywhere, anywhere, vmem),
        scratch_shapes=[
            pltpu.VMEM((2, rows, W), bf16),
            pltpu.VMEM((2, rows, W), bf16),
            pltpu.VMEM((2, rows, W), bf16),
            pltpu.VMEM((2, rows, W), bf16),
            pltpu.VMEM((4, rows, W), bf16),
            pltpu.VMEM((2 * C, 27 * C), bf16),
            pltpu.VMEM((27 * C, wide), f32),
            pltpu.VMEM((4, 3, 3 * C, 3 * C), bf16),
            pltpu.VMEM((2, 27 * cs, wide), f32),
            pltpu.VMEM((2, 6, C, (D + 2) * (H + 2) * W), bf16),
            pltpu.VMEM((6, rows, W), f32),
            pltpu.VMEM((6, C, D * H * W), bf16),
            pltpu.VMEM((2, 6, C, D * H * W), bf16),
            pltpu.VMEM((6, rows, W), bf16),
            pltpu.VMEM((3, 3 * C, D * H * W), f32),
            pltpu.VMEM((2, 3 * C, D * H * W), bf16),
            pltpu.VMEM((2, 9 * C, 3 * C), f32),
            pltpu.VMEM((2, n, 9, cs, wide), f32),
            pltpu.VMEM((2, n, 9, cs, wide), f32),
            dma((2, 6, 2)),
            dma((2, 6, 2)),
            dma((2, 6)),
            dma((2, 6)),
            dma((6,)),
            dma((2, n)),
            dma((2, n)),
            dma((6,)),
            pltpu.VMEM((2, C, D * H * W), bf16),
            dma((3, 2)),
        ],
        compiler_params=pltpu.CompilerParams(
            collective_id=0, has_side_effects=True, vmem_limit_bytes=67043328
        ),
        name="petra",
    )(
        fwd_in.reshape(2, rows, W),
        back_out.reshape(2, rows, W),
        back_grad.reshape(2, rows, W),
        batch_next.reshape(2, rows, W),
        loss_grad.reshape(4, rows, W),
        weights.reshape(2 * C, 27 * C),
    )
    fout, backs, grads, dw = pl.pallas_call(
        write_out,
        out_shape=(pair, pair, pair, share),
        in_specs=[hbm] * 4,
        out_specs=(hbm,) * 4,
        scratch_shapes=[pltpu.VMEM(x.shape, x.dtype) for x in (pair, pair, pair, share)]
        + [dma((2, 4))],
        compiler_params=pltpu.CompilerParams(vmem_limit_bytes=67043328),
        name="write_out",
    )(fout, backs, grads, dw)
    shape = fwd_in.shape
    return fout.reshape(shape), backs.reshape(shape), grads.reshape(shape), dw[None]


def solution(mesh):
    field = P("segment", None, None, "slab", None, None)
    return jax.shard_map(
        functools.partial(local, mesh.shape["segment"], mesh.shape["slab"]),
        mesh=mesh,
        in_specs=(
            field,
            field,
            field,
            P(None, None, "slab", None, None),
            P(None, None, None, "slab", None, None),
            P("segment", None, None, None),
        ),
        out_specs=(field, field, field, P("segment", None, None, "slab")),
        check_vma=False,
    )
```
